32 devices in a mesh: fsdp: 16 (over z, y, core), tp: 2 (over x).
Axes of the slice: x: 2, y: 2, z: 4, core: 2. Of those that a mesh axis runs over, the one named last changes fastest.
Arguments:
- tokens: bfloat16 [16, 1024, 1152], P('fsdp', 'tp'), may hold values from -6 to 6
- condition: bfloat16 [16, 1152], P('fsdp'), may hold values from -3 to 3
- mod_weight: bfloat16 [1152, 6912], P('tp', 'fsdp'), may hold values from -0.088388348 to 0.088388348
- mod_bias: bfloat16 [6912], P('fsdp'), may hold values from -1.5 to 1.5
- qkv_weight: bfloat16 [1152, 3, 1152], P('fsdp', None, 'tp'), may hold values from -0.088388348 to 0.088388348
- qv_bias: bfloat16 [2, 1152], P(None, 'fsdp'), may hold values from -2 to 2
- out_weight: bfloat16 [1152, 1152], P('tp', 'fsdp'), may hold values from -0.75 to 0.75
- out_bias: bfloat16 [1152], P('fsdp'), may hold values from -3 to 3
- up_weight: bfloat16 [1152, 4608], P('fsdp', 'tp'), may hold values from -0.1875 to 0.1875
- up_bias: bfloat16 [4608], P('fsdp'), may hold values from -3 to 3
- down_weight: bfloat16 [4608, 1152], P('tp', 'fsdp'), may hold values from -0.09375 to 0.09375
- down_bias: bfloat16 [1152], P('fsdp'), may hold values from -3 to 3
- cotangent: bfloat16 [16, 1024, 1152], P('fsdp', 'tp'), may hold values from -6 to 6
Outputs:
- result: bfloat16 [16, 1024, 1152], P('fsdp', 'tp')
- tokens_grad: bfloat16 [16, 1024, 1152], P('fsdp', 'tp')
- condition_grad: float32 [16, 1152], P('fsdp', 'tp')
- mod_weight_grad: float32 [1152, 6912], P('tp', 'fsdp')
- mod_bias_grad: float32 [6912], P('fsdp')
- qkv_weight_grad: float32 [1152, 3, 1152], P('fsdp', None, 'tp')
- qv_bias_grad: float32 [2, 1152], P(None, 'fsdp')
- out_weight_grad: float32 [1152, 1152], P('tp', 'fsdp')
- out_bias_grad: float32 [1152], P('fsdp')
- up_weight_grad: float32 [1152, 4608], P('fsdp', 'tp')
- up_bias_grad: float32 [4608], P('fsdp')
- down_weight_grad: float32 [4608, 1152], P('tp', 'fsdp')
- down_bias_grad: float32 [1152], P('fsdp')
The draws below stay inside these ranges and needn't reach their ends.
All inputs are finite; a program needn't handle non-finite values.
Results may differ from the reference program's by a relative error of at most 0.015.
Values may be sent and summed in bfloat16 or wider, within the bound.
A program may use at most 256 MiB of HBM per device.

```python
import math
import jax
import jax.numpy as jnp
from jax import lax

D = 1152
HEADS = 16
HEAD_DIM = 72
FF = 4608
SEQ = 1024
LATENTS = 16


def drawn_draw(key, shape, deviation, bound):
    values = jax.random.normal(key, shape, jnp.float32) * deviation
    return jnp.clip(values, -bound, bound).astype(jnp.bfloat16)


def draw_condition(key, part):
    return drawn_draw(jax.random.fold_in(key, 11), (LATENTS, D), 1.0, 3.0)


def draw_mod_weight(key, part):
    deviation = 1.0 / D ** 0.5
    return drawn_draw(jax.random.fold_in(key, 12), (D, 6 * D), deviation, 3.0 * deviation)


def draw_mod_bias(key, part):
    return drawn_draw(jax.random.fold_in(key, 13), (6 * D,), 0.5, 1.5)


def draw_qkv_weight(key, part):
    deviation = 1.0 / D ** 0.5
    return drawn_draw(jax.random.fold_in(key, 14), (D, 3, D), deviation, 3.0 * deviation)


def shard_levels(own_key, extent, split, smallest, top_value):
    def one(dim, parts):
        heights = jax.random.uniform(jax.random.fold_in(jax.random.fold_in(own_key, 6), dim), (parts,), jnp.float32, smallest / len(split), top_value / len(split))
        return jnp.repeat(jnp.exp(heights), extent[dim] // parts).reshape((-1,) + (1,) * (len(extent) - dim - 1))

    gain = one(*split[0])
    for cut in split[1:]:
        gain = gain * one(*cut)
    return gain


def scatter_about(rng, dims, spread, limit, cuts=(), held_as=jnp.bfloat16):
    entries = spread * jax.random.normal(rng, dims, jnp.float32)
    if cuts:
        entries = entries * shard_levels(rng, dims, cuts, -0.22, 0.18)
    return jnp.clip(entries, -limit, limit).astype(held_as)


def setup_inputs(seed: int = 0) -> dict:
    key_list = jax.random.split(jax.random.key(seed), 14)
    tokens = scatter_about(key_list[0], (LATENTS, SEQ, D), 1.0, 6.0, ((0, 16), (1, 2)))
    condition = draw_condition(jax.random.fold_in(key_list[13], 71), 0)
    mod_weight = draw_mod_weight(jax.random.fold_in(key_list[13], 71), 0)
    mod_bias = draw_mod_bias(jax.random.fold_in(key_list[13], 71), 0)
    qkv_weight = draw_qkv_weight(jax.random.fold_in(key_list[13], 71), 0)
    qv_bias = scatter_about(key_list[5], (2, D), 0.3, 2.0, ((1, 16),))
    out_weight = scatter_about(key_list[6], (D, D), (D // 16) ** -0.5, 0.75, ((0, 2), (1, 16)))
    out_bias = scatter_about(key_list[7], (D,), 0.5, 3.0, ((0, 16),))
    up_weight = scatter_about(key_list[8], (D, FF), D ** -0.5, 0.1875, ((0, 16), (1, 2)))
    up_bias = scatter_about(key_list[9], (FF,), 0.5, 3.0, ((0, 16),))
    down_weight = scatter_about(key_list[10], (FF, D), FF ** -0.5, 0.09375, ((0, 2), (1, 16)))
    down_bias = scatter_about(key_list[11], (D,), 0.5, 3.0, ((0, 16),))
    cotangent = scatter_about(key_list[12], (LATENTS, SEQ, D), 1.0, 6.0, ((0, 16), (1, 2)))
    return {"tokens": tokens, "condition": condition, "mod_weight": mod_weight, "mod_bias": mod_bias, "qkv_weight": qkv_weight, "qv_bias": qv_bias, "out_weight": out_weight, "out_bias": out_bias, "up_weight": up_weight, "up_bias": up_bias, "down_weight": down_weight, "down_bias": down_bias, "cotangent": cotangent}


EPSILON = 1e-06
HIGH = lax.Precision.HIGHEST

@jax.custom_vjp
def low(v):
    return lax.optimization_barrier(v.astype(jnp.bfloat16)).astype(jnp.float32)

@jax.custom_vjp
def low_back(v):
    return v

def low_keep(v):
    return (low(v), None)

def low_pass(kept, grad):
    return (grad,)

def back_keep(v):
    return (v, None)

def back_low(kept, grad):
    return (low(grad),)
low.defvjp(low_keep, low_pass)
low_back.defvjp(back_keep, back_low)

def matmul(left, right):
    return jnp.dot(left, right, precision=HIGH, preferred_element_type=jnp.float32)

def layer_norm(values):
    center = values - lax.optimization_barrier(jnp.mean(values, axis=-1, keepdims=True))
    variance = lax.optimization_barrier(jnp.mean(center * center, axis=-1, keepdims=True))
    return center * lax.rsqrt(variance + EPSILON)

def attention(queries, keys_all, values_all):
    seq_len = queries.shape[1]
    block = min(512, seq_len)
    scaling = 1.0 / math.sqrt(HEAD_DIM)

    def one_block(query_block):
        scores = low_back(scaling * jnp.einsum('hqd,hkd->hqk', query_block, keys_all, precision=HIGH))
        weights = jax.nn.softmax(scores, axis=-1)
        return jnp.einsum('hqk,hkd->hqd', low(weights), values_all, precision=HIGH)
    blocks = queries.reshape(HEADS, seq_len // block, block, HEAD_DIM).transpose(1, 0, 2, 3)
    outputs = lax.map(jax.checkpoint(one_block), blocks)
    return outputs.transpose(1, 0, 2, 3).reshape(HEADS, seq_len, HEAD_DIM)

def layer(params, token_rows, cond_row):
    mod_weight, mod_bias, qkv_weight, qv_bias, out_weight, out_bias, up_weight, up_bias, down_weight, down_bias = params
    seq_len = token_rows.shape[0]
    silu_low = low(jax.nn.silu(cond_row))
    modulation = matmul(silu_low[None, :], mod_weight)[0] + mod_bias
    pieces = modulation.reshape(6, D)
    shift_one = pieces[0]
    scale_one = pieces[1]
    gate_one = pieces[2]
    shift_two = pieces[3]
    scale_two = pieces[4]
    gate_two = pieces[5]
    normed_one = layer_norm(token_rows)
    hidden_one = low(normed_one * (1.0 + scale_one) + shift_one)
    bias_rows = jnp.stack([qv_bias[0], jnp.zeros_like(qv_bias[0]), qv_bias[1]])
    projected = matmul(hidden_one, qkv_weight.reshape(D, 3 * D)).reshape(seq_len, 3, D) + bias_rows[None]
    projected = low_back(low(projected))
    heads = projected.reshape(seq_len, 3, HEADS, HEAD_DIM).transpose(1, 2, 0, 3)
    attended = attention(heads[0], heads[1], heads[2])
    attended = attended.transpose(1, 0, 2).reshape(seq_len, D)
    attended = low_back(low(attended))
    branch_one = low_back(matmul(attended, out_weight) + out_bias)
    middle = token_rows + gate_one * branch_one
    normed_two = layer_norm(middle)
    hidden_two = low(normed_two * (1.0 + scale_two) + shift_two)
    before = low_back(matmul(hidden_two, up_weight) + up_bias)
    activated = low(jax.nn.gelu(before, approximate=True))
    branch_two = low_back(matmul(activated, down_weight) + down_bias)
    return middle + gate_two * branch_two

def reference(tokens, condition, mod_weight, mod_bias, qkv_weight, qv_bias, out_weight, out_bias, up_weight, up_bias, down_weight, down_bias, cotangent):
    params = tuple((param.astype(jnp.float32) for param in (mod_weight, mod_bias, qkv_weight, qv_bias, out_weight, out_bias, up_weight, up_bias, down_weight, down_bias)))

    def step(totals, inputs):
        token_rows, cond_row, grad_rows = inputs
        outcome, pull = jax.vjp(layer, params, token_rows, cond_row)
        grad_params, grad_tokens, grad_cond = pull(grad_rows)
        totals = jax.tree.map(lambda left, right: left + right, totals, grad_params)
        return (totals, (outcome.astype(jnp.bfloat16), grad_tokens.astype(jnp.bfloat16), grad_cond))
    zeros = tuple((jnp.zeros_like(param) for param in params))
    totals, (outputs, input_grads, cond_grads) = lax.scan(step, zeros, (tokens.astype(jnp.float32), condition.astype(jnp.float32), cotangent.astype(jnp.float32)))
    return (outputs, input_grads, cond_grads, totals[0], totals[1], totals[2], totals[3], totals[4], totals[5], totals[6], totals[7], totals[8], totals[9])
```

```python
import math

import jax
import jax.numpy as jnp
from jax import lax
from jax.sharding import PartitionSpec as P

HEAD_DIM = 72


EPSILON = 1e-06
HIGH = lax.Precision.HIGHEST


def normalize(values):
    center = values - jnp.mean(values, axis=-1, keepdims=True)
    variance = jnp.mean(center * center, axis=-1, keepdims=True)
    inverse = lax.rsqrt(variance + EPSILON)
    return (center * inverse, inverse)


def norm_back(grad_norm, normed, inverse):
    first_mean = jnp.mean(grad_norm, axis=-1, keepdims=True)
    second_mean = jnp.mean(grad_norm * normed, axis=-1, keepdims=True)
    return inverse * (grad_norm - first_mean - normed * second_mean)


def inner_rows(left, right):
    return lax.dot_general(
        left, right, (((0,), (0,)), ((), ())), preferred_element_type=jnp.float32
    )


def outer_cols(left, right):
    return lax.dot_general(
        left, right, (((1,), (1,)), ((), ())), preferred_element_type=jnp.float32
    )


def gelu_tanh(values):
    return jax.nn.gelu(values, approximate=True)


def to_heads(flat, head_count):
    return flat.reshape(flat.shape[0], head_count, HEAD_DIM).transpose(1, 0, 2)


def from_heads(stacked):
    return stacked.transpose(1, 0, 2).reshape(stacked.shape[1], stacked.shape[0] * HEAD_DIM)


def swap(values):
    return lax.ppermute(values, "tp", [(0, 1), (1, 0)])


def gather_rows(values, tp_count):
    if tp_count == 2:
        return jnp.concatenate([values, swap(values)], axis=0)
    return lax.all_gather(values, "tp", axis=0, tiled=True)


def scatter_rows(left, right, contract, tp_count):
    if tp_count == 2:
        half = left.shape[0] // 2
        sent = swap(contract(left[half:], right).astype(jnp.bfloat16))
        return contract(left[:half], right) + sent.astype(jnp.float32)
    return lax.psum_scatter(
        contract(left, right).astype(jnp.bfloat16), "tp", scatter_dimension=0, tiled=True
    ).astype(jnp.float32)


def sum_pair(values, tp_count):
    if tp_count == 2:
        return values + swap(values)
    return lax.psum(values, "tp")


def plain(left, right):
    return jnp.dot(left, right, preferred_element_type=jnp.float32)


def reduce_grad(term, axis):
    return lax.psum_scatter(
        term.astype(jnp.bfloat16), "fsdp", scatter_dimension=axis, tiled=True
    )


def gather_small(flat):
    size = flat.shape[0]
    padded = -(-size // 1024) * 1024
    block = jnp.pad(flat, (0, padded - size)).reshape(8, padded // 8)
    return lax.all_gather(block, "fsdp", axis=0, tiled=True).reshape(-1, padded)[:, :size]


def trade(rows):
    return lax.all_to_all(rows, "fsdp", split_axis=0, concat_axis=0, tiled=True)


def shards(
    tokens,
    condition,
    mod_weight,
    mod_bias,
    qkv_weight,
    qv_bias,
    out_weight,
    out_bias,
    up_weight,
    up_bias,
    down_weight,
    down_bias,
    cotangent,
):
    tp_count = lax.axis_size("tp")
    tp_place = lax.axis_index("tp")
    fsdp_count = lax.axis_size("fsdp")
    local_rows = tokens.shape[1]
    width = tokens.shape[2]
    seq_len = local_rows * tp_count
    share = width // tp_count
    thin = width // fsdp_count
    hidden_thin = up_bias.shape[0]
    hidden_full = hidden_thin * fsdp_count
    mod_thin = mod_bias.shape[0]
    small = gather_small(
        jnp.concatenate([condition[0], qv_bias.reshape(-1), out_bias, up_bias, down_bias])
    ).astype(jnp.float32)
    qkv_full = lax.all_gather(qkv_weight, "fsdp", axis=0, tiled=True)
    out_full = lax.all_gather(out_weight, "fsdp", axis=1, tiled=True)
    up_full = lax.all_gather(up_weight, "fsdp", axis=0, tiled=True)
    down_full = lax.all_gather(down_weight, "fsdp", axis=1, tiled=True)
    cond_all = small[:, :width]
    spot = width
    qv_full = (
        small[:, spot : spot + 2 * thin]
        .reshape(fsdp_count, 2, thin)
        .transpose(1, 0, 2)
        .reshape(2, width)
    )
    spot += 2 * thin
    out_shift = small[:, spot : spot + thin].reshape(-1)
    spot += thin
    up_shift = small[:, spot : spot + hidden_thin].reshape(-1)
    spot += hidden_thin
    down_shift = small[:, spot : spot + thin].reshape(-1)
    head_cols = qkv_full.shape[2]
    head_count = head_cols // HEAD_DIM
    hidden_cols = up_full.shape[1]
    cond_part = lax.dynamic_slice_in_dim(cond_all, tp_place * share, share, 1)
    silu_low = jax.nn.silu(cond_part).astype(jnp.bfloat16)
    partial_mod = jnp.dot(silu_low, mod_weight, preferred_element_type=jnp.float32)
    modulation = trade(sum_pair(partial_mod, tp_count) + mod_bias.astype(jnp.float32)).reshape(-1)
    pieces = modulation.reshape(6, width)
    shift_one = pieces[0]
    scale_one = pieces[1]
    gate_one = pieces[2]
    shift_two = pieces[3]
    scale_two = pieces[4]
    gate_two = pieces[5]
    rows_in = tokens[0].astype(jnp.float32)
    normed_one, inverse_one = normalize(rows_in)
    hidden_one = gather_rows(
        (normed_one * (1.0 + scale_one) + shift_one).astype(jnp.bfloat16), tp_count
    )
    qkv_matrix = qkv_full.reshape(width, 3 * head_cols)
    projected = plain(hidden_one, qkv_matrix).reshape(seq_len, 3, head_cols)
    qv_local = lax.dynamic_slice_in_dim(qv_full, tp_place * head_cols, head_cols, 1)
    queries = to_heads((projected[:, 0] + qv_local[0]).astype(jnp.bfloat16), head_count)
    keys_all = to_heads(projected[:, 1].astype(jnp.bfloat16), head_count)
    values_all = to_heads((projected[:, 2] + qv_local[1]).astype(jnp.bfloat16), head_count)
    grad_rows = cotangent[0].astype(jnp.float32)
    grad_two_own = (grad_rows * gate_two).astype(jnp.bfloat16)
    grad_branch_two = gather_rows(grad_two_own, tp_count)
    block = min(512, seq_len)
    block_count = seq_len // block
    scaling = 1.0 / math.sqrt(HEAD_DIM)
    query_blocks = queries.reshape(head_count, block_count, block, HEAD_DIM).transpose(1, 0, 2, 3)

    def attend(query_block):
        scores = (
            jnp.einsum("hqd,hkd->hqk", query_block, keys_all, preferred_element_type=jnp.float32)
            * scaling
        )
        highest = jnp.max(scores, axis=-1, keepdims=True)
        raised = jnp.exp(scores - highest)
        totals = jnp.sum(raised, axis=-1, keepdims=True)
        weights = (raised / totals).astype(jnp.bfloat16)
        output = jnp.einsum("hqk,hkd->hqd", weights, values_all, preferred_element_type=jnp.float32)
        return (output, (highest + jnp.log(totals))[..., 0])

    attended_blocks, log_totals = lax.map(attend, query_blocks)
    attended = attended_blocks.transpose(1, 0, 2, 3).reshape(head_count, seq_len, HEAD_DIM)
    attended_low = from_heads(attended).astype(jnp.bfloat16)
    branch_one = scatter_rows(attended_low, out_full, plain, tp_count) + out_shift
    middle = rows_in + gate_one * branch_one
    normed_two, inverse_two = normalize(middle)
    hidden_two = gather_rows(
        (normed_two * (1.0 + scale_two) + shift_two).astype(jnp.bfloat16), tp_count
    )
    up_local = lax.dynamic_slice_in_dim(up_shift, tp_place * hidden_cols, hidden_cols)
    before = plain(hidden_two, up_full) + up_local
    activated, gelu_pull = jax.vjp(gelu_tanh, before)
    activated_low = activated.astype(jnp.bfloat16)
    grad_before = gelu_pull(outer_cols(grad_branch_two, down_full))[0].astype(jnp.bfloat16)
    grad_hidden_two = scatter_rows(grad_before, up_full, outer_cols, tp_count)
    branch_two = scatter_rows(activated_low, down_full, plain, tp_count) + down_shift
    outcome = (middle + gate_two * branch_two).astype(jnp.bfloat16)
    grad_gate_two = jnp.sum(grad_rows * branch_two, axis=0)
    down_bias_part = jnp.sum(grad_two_own.astype(jnp.float32), axis=0)
    down_grad = reduce_grad(inner_rows(activated_low, grad_branch_two), 1)
    up_bias_part = jnp.sum(grad_before.astype(jnp.float32), axis=0)
    up_grad = reduce_grad(inner_rows(hidden_two, grad_before), 0)
    grad_scale_two = jnp.sum(grad_hidden_two * normed_two, axis=0)
    grad_shift_two = jnp.sum(grad_hidden_two, axis=0)
    grad_middle = grad_rows + norm_back(
        grad_hidden_two * (1.0 + scale_two), normed_two, inverse_two
    )
    grad_gate_one = jnp.sum(grad_middle * branch_one, axis=0)
    grad_one_own = (grad_middle * gate_one).astype(jnp.bfloat16)
    grad_branch_one = gather_rows(grad_one_own, tp_count)
    out_bias_part = jnp.sum(grad_one_own.astype(jnp.float32), axis=0)
    out_grad = reduce_grad(inner_rows(attended_low, grad_branch_one), 1)
    grad_attended = outer_cols(grad_branch_one, out_full).astype(jnp.bfloat16)
    grad_blocks = (
        to_heads(grad_attended, head_count)
        .reshape(head_count, block_count, block, HEAD_DIM)
        .transpose(1, 0, 2, 3)
    )

    def attend_back(carry, inputs):
        grad_keys, grad_values = carry
        query_block, log_block, grad_block = inputs
        scores = (
            jnp.einsum("hqd,hkd->hqk", query_block, keys_all, preferred_element_type=jnp.float32)
            * scaling
        )
        weights = jnp.exp(scores - log_block[..., None])
        grad_weights = jnp.einsum(
            "hqd,hkd->hqk", grad_block, values_all, preferred_element_type=jnp.float32
        )
        centered = jnp.sum(weights * grad_weights, axis=-1, keepdims=True)
        grad_scores = (weights * (grad_weights - centered)).astype(jnp.bfloat16)
        grad_query = (
            jnp.einsum("hqk,hkd->hqd", grad_scores, keys_all, preferred_element_type=jnp.float32)
            * scaling
        )
        grad_keys = (
            grad_keys
            + jnp.einsum(
                "hqk,hqd->hkd", grad_scores, query_block, preferred_element_type=jnp.float32
            )
            * scaling
        )
        grad_values = grad_values + jnp.einsum(
            "hqk,hqd->hkd",
            weights.astype(jnp.bfloat16),
            grad_block,
            preferred_element_type=jnp.float32,
        )
        return ((grad_keys, grad_values), grad_query)

    zero_heads = jnp.zeros((head_count, seq_len, HEAD_DIM), jnp.float32)
    (grad_keys, grad_values), grad_query_blocks = lax.scan(
        attend_back, (zero_heads, zero_heads), (query_blocks, log_totals, grad_blocks)
    )
    grad_queries = grad_query_blocks.transpose(1, 0, 2, 3).reshape(head_count, seq_len, HEAD_DIM)
    grad_projected = jnp.stack(
        [from_heads(grad_queries), from_heads(grad_keys), from_heads(grad_values)], axis=1
    ).astype(jnp.bfloat16)
    grad_projected, down_grad, up_grad, out_grad = lax.optimization_barrier(
        (grad_projected, down_grad, up_grad, out_grad)
    )
    qv_bias_part = jnp.sum(grad_projected[:, 0::2].astype(jnp.float32), axis=0)
    grad_flat = grad_projected.reshape(seq_len, 3 * head_cols)
    grad_hidden_one = scatter_rows(grad_flat, qkv_matrix, outer_cols, tp_count)
    qkv_grad = reduce_grad(inner_rows(hidden_one, grad_flat).reshape(width, 3, head_cols), 0)
    grad_scale_one = jnp.sum(grad_hidden_one * normed_one, axis=0)
    grad_shift_one = jnp.sum(grad_hidden_one, axis=0)
    grad_tokens = grad_middle + norm_back(
        grad_hidden_one * (1.0 + scale_one), normed_one, inverse_one
    )
    grad_mod_part = jnp.concatenate(
        [
            grad_shift_one,
            grad_scale_one,
            grad_gate_one,
            grad_shift_two,
            grad_scale_two,
            grad_gate_two,
        ]
    )
    qv_padded = lax.dynamic_update_slice_in_dim(
        jnp.zeros((2, width), jnp.float32), qv_bias_part, tp_place * head_cols, 1
    )
    up_padded = lax.dynamic_update_slice_in_dim(
        jnp.zeros((hidden_full,), jnp.float32), up_bias_part, tp_place * hidden_cols, 0
    )
    packed = jnp.concatenate(
        [
            grad_mod_part.reshape(fsdp_count, mod_thin),
            qv_padded.reshape(2, fsdp_count, thin)
            .transpose(1, 0, 2)
            .reshape(fsdp_count, 2 * thin),
            out_bias_part.reshape(fsdp_count, thin),
            up_padded.reshape(fsdp_count, hidden_thin),
            down_bias_part.reshape(fsdp_count, thin),
        ],
        axis=1,
    )
    traded = sum_pair(trade(packed), tp_count)
    totals = jnp.sum(traded, axis=0)
    grad_mod = traded[:, :mod_thin]
    mod_weight_grad = lax.dot_general(
        silu_low.astype(jnp.float32), grad_mod, (((0,), (0,)), ((), ())), precision=HIGH
    )
    silu_parts = lax.dot_general(
        grad_mod, mod_weight.astype(jnp.float32), (((1,), (1,)), ((), ())), precision=HIGH
    )
    grad_silu = jnp.sum(trade(silu_parts), axis=0)
    cond_row = condition[0].astype(jnp.float32)
    own_part = lax.dynamic_slice_in_dim(cond_row, tp_place * share, share)
    cond_grad = jax.vjp(jax.nn.silu, own_part)[1](grad_silu)[0][None, :]
    spot = mod_thin
    qv_bias_grad = totals[spot : spot + 2 * thin].reshape(2, thin)
    spot += 2 * thin
    out_bias_grad = totals[spot : spot + thin]
    spot += thin
    up_bias_grad = totals[spot : spot + hidden_thin]
    spot += hidden_thin
    down_bias_grad = totals[spot : spot + thin]
    return (
        outcome[None],
        grad_tokens.astype(jnp.bfloat16)[None],
        cond_grad,
        mod_weight_grad,
        totals[:mod_thin],
        qkv_grad.astype(jnp.float32),
        qv_bias_grad,
        out_grad.astype(jnp.float32),
        out_bias_grad,
        up_grad.astype(jnp.float32),
        up_bias_grad,
        down_grad.astype(jnp.float32),
        down_bias_grad,
    )


def solution(mesh):
    return jax.shard_map(
        shards,
        mesh=mesh,
        in_specs=(
            P("fsdp", "tp", None),
            P("fsdp", None),
            P("tp", "fsdp"),
            P("fsdp"),
            P("fsdp", None, "tp"),
            P(None, "fsdp"),
            P("tp", "fsdp"),
            P("fsdp"),
            P("fsdp", "tp"),
            P("fsdp"),
            P("tp", "fsdp"),
            P("fsdp"),
            P("fsdp", "tp", None),
        ),
        out_specs=(
            P("fsdp", "tp", None),
            P("fsdp", "tp", None),
            P("fsdp", "tp"),
            P("tp", "fsdp"),
            P("fsdp"),
            P("fsdp", None, "tp"),
            P(None, "fsdp"),
            P("tp", "fsdp"),
            P("fsdp"),
            P("fsdp", "tp"),
            P("fsdp"),
            P("tp", "fsdp"),
            P("fsdp"),
        ),
        check_vma=False,
    )
```
